32 devices in a mesh: row: 4 (over y, core), col: 8 (over z, x).
Axes of the slice: x: 2, y: 2, z: 4, core: 2. Of those that a mesh axis runs over, the one named last changes fastest.
Arguments:
- fock: float32 [2, 8192, 8192], P(None, 'row', 'col'), may hold values from -1.1875 to 1.1875, as said below
- density: float32 [2, 8192, 8192], P(None, 'row', 'col'), may hold values from -1.09375 to 1.09375, as said below
- probe: float32 [2, 8192, 128], P(None, 'col'), may hold values from -6 to 6
Outputs:
- propagated: float32 [2, 8192, 128], P(None, 'col')
The draws below stay inside these ranges and needn't reach their ends.
Inputs may be any that keep to these rules, and one draw needn't show every extreme that they name: Hermitian: fock[0] is symmetric and fock[1] antisymmetric, exactly. Hermitian: density[0] is symmetric and density[1] antisymmetric, exactly.
All inputs are finite; a program needn't handle non-finite values.
Results may differ from the reference program's by a relative error of at most 0.00011.
Values sent between devices are 32-bit elements; how exact they have to be, the bound alone decides.
A program may use at most 128 MiB of HBM per device.

```python
import jax
import jax.numpy as jnp
from jax import lax

N = 8192
M = 128
ORDER = 1


def hermitian(key, spread):
    key_real, key_imag = jax.random.split(key, 2)
    real_base = jnp.clip(jax.random.normal(key_real, (N, N), jnp.float32), -6.0, 6.0)
    imag_base = jnp.clip(jax.random.normal(key_imag, (N, N), jnp.float32), -6.0, 6.0)
    factor = spread / jnp.sqrt(2.0 * N)
    real_part = (real_base + real_base.T) * factor
    imag_part = (imag_base - imag_base.T) * factor
    return jnp.stack([real_part, imag_part])


def draw_fock(key, part):
    return hermitian(jax.random.fold_in(key, 11), 2.0)


def draw_density(key, part):
    return hermitian(jax.random.fold_in(key, 23), 1.0)


def block_scale(rng, dims, cuts, smallest, high):
    factor_of, own = 1.0, jax.random.fold_in(rng, 6)
    for position, parts in cuts:
        draws = jnp.exp(jax.random.uniform(jax.random.fold_in(own, position), (parts,), jnp.float32, smallest / len(cuts), high / len(cuts)))
        factor_of = factor_of * jnp.repeat(draws, dims[position] // parts).reshape([-1 if axis == position else 1 for axis in range(len(dims))])
    return factor_of


def gaussian(key, dims, scale, reach, cuts=(), kind=jnp.bfloat16):
    entries = jax.random.normal(key, dims, jnp.float32) * scale
    if len(cuts) > 0:
        entries = block_scale(key, dims, cuts, -0.22, 0.18) * entries
    return jnp.clip(entries, min=-reach, max=reach).astype(kind)


def setup_inputs(seed: int = 0) -> dict:
    streams_of = jax.random.split(jax.random.key(seed), 4)
    fock = draw_fock(jax.random.fold_in(streams_of[3], 71), 0)
    density = draw_density(jax.random.fold_in(streams_of[3], 71), 0)
    probe = gaussian(streams_of[2], (2, N, M), 1.0, 6.0, ((1, 8),), jnp.float32)
    return {"fock": fock, "density": density, "probe": probe}


time_step = 0.5


def complex_product(matrix, vector):
    hp = lax.Precision.HIGHEST
    real_part = jnp.dot(matrix[0], vector[0], precision=hp, preferred_element_type=jnp.float32) - jnp.dot(matrix[1], vector[1], precision=hp, preferred_element_type=jnp.float32)
    imag_part = jnp.dot(matrix[0], vector[1], precision=hp, preferred_element_type=jnp.float32) + jnp.dot(matrix[1], vector[0], precision=hp, preferred_element_type=jnp.float32)
    return jnp.stack([real_part, imag_part])


def times_imag(vector, factor):
    return jnp.stack([-factor * vector[1], factor * vector[0]])


def series(fock, start, sign):
    current = start
    total = start
    for degree in range(1, ORDER + 1):
        current = times_imag(complex_product(fock, current), sign * time_step / degree)
        total = total + current
    return total


def reference(fock, density, probe):
    first = series(fock, probe, 1.0)
    second = complex_product(density, first)
    return series(fock, second, -1.0)
```

```python
import functools

import jax
import jax.numpy as jnp
from jax import lax
from jax.experimental import pallas as pl
from jax.experimental.pallas import tpu as pltpu
from jax.sharding import PartitionSpec as P

time_step = 0.5
MESH = pl.DeviceIdType.MESH


def split(value):
    high = value.astype(jnp.bfloat16)
    return high, (value - high.astype(jnp.float32)).astype(jnp.bfloat16)


def dot3(left, right):
    dot = functools.partial(jnp.dot, preferred_element_type=jnp.float32)
    return dot(left[0], right[0]) + (dot(left[0], right[1]) + dot(left[1], right[0]))


def kernel(
    nr, nc, fock_hbm, density_hbm, probe_ref, out_ref,
    fock, density, high, low, base,
    send1, recv1, gather1, turned, flat, recv2, gather2, send3, recv3, moved, gather4,
    fock_sem, density_sem, own_sem,
    s1, r1, s2, r2, s3, r3, s4, r4, s5, r5, s6, r6, s7, r7,
):
    r = lax.axis_index("row")
    c = lax.axis_index("col")
    rows = fock.shape[1]
    cols = fock.shape[2]
    m = probe_ref.shape[2]
    s = rows // nc

    def at(block):
        return pl.ds(pl.multiple_of(block * s, s), s)

    def peer_to(me, d, n):
        return lax.rem(me + 1 + d, n)

    def peer_from(me, d, n):
        return lax.rem(me + 2 * n - 1 - d, n)

    def fock_load(d):
        block = peer_to(c, d, nc)
        return pltpu.make_async_copy(
            fock_hbm.at[:, at(block), :], fock.at[:, at(block), :], fock_sem.at[d]
        )

    def density_load(d):
        block = peer_from(c, lax.rem(d + nc - 1, nc), nc)
        return pltpu.make_async_copy(
            density_hbm.at[:, at(block), :], density.at[:, at(block), :], density_sem.at[d]
        )

    def each(n, body):
        def step(d, carry):
            body(d)
            return carry

        lax.fori_loop(0, n, step, 0)

    each(nc, lambda d: fock_load(d).start())
    each(nc, lambda d: density_load(d).start())

    mine = nc * r + c
    wanted = nr * c + r
    goal = (lax.rem(mine, nr), lax.div(mine, nr))
    stays = mine == wanted

    barrier = pltpu.get_barrier_semaphore()

    def greet(where):
        pl.semaphore_signal(barrier, inc=1, device_id=where, device_id_type=MESH)

    def greet_next(d):
        other = lax.rem(mine + 1 + d, nr * nc)
        greet((lax.div(other, nc), lax.rem(other, nc)))

    each(nr * nc - 1, greet_next)

    base[:, :m] = probe_ref[0]
    base[:, m:] = probe_ref[1]
    top, rest = split(base[...])
    high[...] = top
    low[...] = rest

    pl.semaphore_wait(barrier, nr * nc - 1)

    def col_copy(d, source, target, ssem, rsem):
        return pltpu.make_async_remote_copy(
            src_ref=source, dst_ref=target.at[d], send_sem=ssem.at[d], recv_sem=rsem.at[d],
            device_id=(r, peer_to(c, d, nc)), device_id_type=MESH,
        )

    def row_copy(d, source, target, ssem, rsem):
        return pltpu.make_async_remote_copy(
            src_ref=source, dst_ref=target.at[d], send_sem=ssem.at[d], recv_sem=rsem.at[d],
            device_id=(peer_to(r, d, nr), c), device_id_type=MESH,
        )

    def forward(block, factor):
        right = (high[...], low[...])
        one = dot3(split(fock[0, at(block), :]), right)
        two = dot3(split(fock[1, at(block), :]), right)
        real = one[:, :m] - two[:, m:]
        imag = one[:, m:] + two[:, :m]
        piece = nc * r + block
        weight = jnp.where(lax.div(piece, nr) == c, 1.0, 0.0).astype(jnp.float32)
        own = base[at(lax.rem(piece, nr)), :] * weight
        return own[:, :m] - factor * imag, own[:, m:] + factor * real

    def forward_reduce(factor, load, send, recv, ssem, rsem):
        def step(d):
            if load:
                fock_load(d).wait()
            real, imag = forward(peer_to(c, d, nc), factor)
            send[d, :, :m] = real
            send[d, :, m:] = imag
            col_copy(d, send.at[d], recv, ssem, rsem).start()

        each(nc - 1, step)
        if load:
            fock_load(nc - 1).wait()
        real, imag = forward(c, factor)
        recv[nc - 1, :, :m] = real
        recv[nc - 1, :, m:] = imag

        def take(d):
            col_copy(d, send.at[d], recv, ssem, rsem).wait_recv()
            recv[nc - 1] += recv[d]

        each(nc - 1, take)

    forward_reduce(time_step, True, send1, recv1, s1, r1)

    gather1[nc - 1] = recv1[nc - 1]
    each(nc - 1, lambda d: col_copy(d, gather1.at[nc - 1], gather1, s2, r2).start())

    def backward(slot, d):
        density_load(d).wait()
        block = peer_from(c, slot, nc)
        left = split(gather1[slot].T)
        one = dot3(left, split(density[0, at(block), :]))
        two = dot3(left, split(density[1, at(block), :]))
        return one[:m] + two[m:], one[m:] - two[:m]

    real, imag = backward(nc - 1, 0)
    turned[:m] = real
    turned[m:] = imag

    def gathered(d):
        col_copy(d, gather1.at[nc - 1], gather1, s2, r2).wait_recv()
        real, imag = backward(d, d + 1)
        turned[:m] += real
        turned[m:] += imag

    each(nc - 1, gathered)
    flat[...] = turned[...].T

    each(nr - 1, lambda d: row_copy(d, flat.at[at(peer_to(r, d, nr)), :], recv2, s3, r3).start())
    recv2[nr - 1] = flat[at(r), :]

    def take_row(d):
        row_copy(d, flat.at[at(peer_to(r, d, nr)), :], recv2, s3, r3).wait_recv()
        recv2[nr - 1] += recv2[d]

    each(nr - 1, take_row)

    gather2[nr - 1] = recv2[nr - 1]
    each(nr - 1, lambda d: row_copy(d, gather2.at[nr - 1], gather2, s4, r4).start())

    def place(slot):
        value = gather2[slot]
        where = at(peer_from(r, slot, nr))
        top, rest = split(value)
        base[where, :] = value
        high[where, :] = top
        low[where, :] = rest

    place(nr - 1)

    def take_vector(d):
        row_copy(d, gather2.at[nr - 1], gather2, s4, r4).wait_recv()
        place(d)

    each(nr - 1, take_vector)

    forward_reduce(-time_step, False, send3, recv3, s5, r5)

    moved[...] = recv3[nc - 1]

    def move():
        return pltpu.make_async_remote_copy(
            src_ref=moved, dst_ref=gather4.at[nr - 1], send_sem=s6.at[0], recv_sem=r6.at[0],
            device_id=goal, device_id_type=MESH,
        )

    def stay():
        return pltpu.make_async_copy(moved, gather4.at[nr - 1], own_sem.at[0])

    @pl.when(stays)
    def _():
        stay().start()
        stay().wait()

    @pl.when(jnp.logical_not(stays))
    def _():
        move().start()
        move().wait()

    each(nr - 1, lambda d: row_copy(d, gather4.at[nr - 1], gather4, s7, r7).start())

    def emit(slot):
        where = at(peer_from(r, slot, nr))
        out_ref[0, where, :] = gather4[slot, :, :m]
        out_ref[1, where, :] = gather4[slot, :, m:]

    emit(nr - 1)

    def take_out(d):
        row_copy(d, gather4.at[nr - 1], gather4, s7, r7).wait_recv()
        emit(d)

    each(nr - 1, take_out)

    def drain_col(d):
        col_copy(d, send1.at[d], recv1, s1, r1).wait_send()
        col_copy(d, gather1.at[nc - 1], gather1, s2, r2).wait_send()
        col_copy(d, send3.at[d], recv3, s5, r5).wait_send()

    def drain_row(d):
        row_copy(d, flat.at[at(peer_to(r, d, nr)), :], recv2, s3, r3).wait_send()
        row_copy(d, gather2.at[nr - 1], gather2, s4, r4).wait_send()
        row_copy(d, gather4.at[nr - 1], gather4, s7, r7).wait_send()

    each(nc - 1, drain_col)
    each(nr - 1, drain_row)


def solution(mesh):
    nr = mesh.shape["row"]
    nc = mesh.shape["col"]

    def shards(fock, density, probe):
        _, rows, cols = fock.shape
        m = probe.shape[2]
        s = rows // nc
        f32 = jnp.float32
        vmem = pltpu.VMEM
        sem = pltpu.SemaphoreType.DMA
        many, few = (nc, s, 2 * m), (nr, s, 2 * m)
        return pl.pallas_call(
            functools.partial(kernel, nr, nc),
            out_shape=jax.ShapeDtypeStruct(probe.shape, f32),
            in_specs=[
                pl.BlockSpec(memory_space=pl.ANY),
                pl.BlockSpec(memory_space=pl.ANY),
                pl.BlockSpec(memory_space=pltpu.VMEM),
            ],
            out_specs=pl.BlockSpec(memory_space=pltpu.VMEM),
            scratch_shapes=[
                vmem(fock.shape, f32),
                vmem(density.shape, f32),
                vmem((cols, 2 * m), jnp.bfloat16),
                vmem((cols, 2 * m), jnp.bfloat16),
                vmem((cols, 2 * m), f32),
                vmem(many, f32),
                vmem(many, f32),
                vmem(many, f32),
                vmem((2 * m, cols), f32),
                vmem((cols, 2 * m), f32),
                vmem(few, f32),
                vmem(few, f32),
                vmem(many, f32),
                vmem(many, f32),
                vmem((s, 2 * m), f32),
                vmem(few, f32),
                sem((nc,)),
                sem((nc,)),
                sem((1,)),
                *[sem((nc,))] * 14,
            ],
            compiler_params=pltpu.CompilerParams(
                collective_id=0, has_side_effects=True, vmem_limit_bytes=62 * 1024 * 1024
            ),
            name="propagate",
        )(fock, density, probe)

    return jax.shard_map(
        shards,
        mesh=mesh,
        in_specs=(P(None, "row", "col"), P(None, "row", "col"), P(None, "col", None)),
        out_specs=P(None, "col", None),
        check_vma=False,
    )
```

```python
import functools

import jax
import jax.numpy as jnp
from jax import lax
from jax.experimental import pallas as pl
from jax.experimental.pallas import tpu as pltpu
from jax.sharding import PartitionSpec as P

time_step = 0.5
MESH = pl.DeviceIdType.MESH


def split(value):
    high = value.astype(jnp.bfloat16)
    return high, (value - high.astype(jnp.float32)).astype(jnp.bfloat16)


def dot3(left, right):
    dot = functools.partial(jnp.dot, preferred_element_type=jnp.float32)
    return dot(left[0], right[0]) + (dot(left[0], right[1]) + dot(left[1], right[0]))


def kernel(
    nr, nc, fock_hbm, density_hbm, probe_ref, out_ref,
    fock, density, high, low, base,
    send1, recv1, gather1, turned, flat, recv2, gather2, send3, recv3, moved, gather4,
    fock_sem, density_sem, own_sem,
    s1, r1, s2, r2, s3, r3, s4, r4, s5, r5, s6, r6, s7, r7,
):
    r = lax.axis_index("row")
    c = lax.axis_index("col")
    rows = fock.shape[1]
    cols = fock.shape[2]
    m = probe_ref.shape[2]
    s = rows // nc
    half = nc // 2
    side = lax.div(c, half)
    spot = lax.rem(c, half)

    def block_to(e):
        return lax.rem(side + 1 + e // half, 2) * half + lax.rem(spot + 1 + e % half, half)

    def block_from(e):
        return lax.rem(side + 1 + e // half, 2) * half + lax.rem(spot + half - 1 - e % half, half)

    def near(e):
        return side * half + lax.rem(spot + 1 + e % half, half)

    across = lax.rem(side + 1, 2) * half + spot

    def at(block):
        return pl.ds(pl.multiple_of(block * s, s), s)

    def peer_to(me, d, n):
        return lax.rem(me + 1 + d, n)

    def peer_from(me, d, n):
        return lax.rem(me + 2 * n - 1 - d, n)

    def fock_load(d):
        block = block_to(d)
        return pltpu.make_async_copy(
            fock_hbm.at[:, at(block), :], fock.at[:, at(block), :], fock_sem.at[d]
        )

    def density_load(d):
        block = block_from(d)
        return pltpu.make_async_copy(
            density_hbm.at[:, at(block), :], density.at[:, at(block), :], density_sem.at[d]
        )

    def each(n, body):
        def step(d, carry):
            body(d)
            return carry

        lax.fori_loop(0, n, step, 0)

    each(nc, lambda d: fock_load(d).start())
    density_load(nc - 1).start()
    density_load(half - 1).start()
    each(half - 1, lambda d: density_load(half + d).start())
    each(half - 1, lambda d: density_load(d).start())

    mine = nc * r + c
    wanted = nr * c + r
    goal = (lax.rem(mine, nr), lax.div(mine, nr))
    stays = mine == wanted

    barrier = pltpu.get_barrier_semaphore()

    def greet(where):
        pl.semaphore_signal(barrier, inc=1, device_id=where, device_id_type=MESH)

    def greet_next(d):
        other = lax.rem(mine + 1 + d, nr * nc)
        greet((lax.div(other, nc), lax.rem(other, nc)))

    each(nr * nc - 1, greet_next)

    base[:, :m] = probe_ref[0]
    base[:, m:] = probe_ref[1]
    top, rest = split(base[...])
    high[...] = top
    low[...] = rest

    pl.semaphore_wait(barrier, nr * nc - 1)

    def col_copy(e, where, source, target, ssem, rsem):
        return pltpu.make_async_remote_copy(
            src_ref=source, dst_ref=target.at[e], send_sem=ssem.at[e], recv_sem=rsem.at[e],
            device_id=(r, where), device_id_type=MESH,
        )

    def row_copy(d, source, target, ssem, rsem):
        return pltpu.make_async_remote_copy(
            src_ref=source, dst_ref=target.at[d], send_sem=ssem.at[d], recv_sem=rsem.at[d],
            device_id=(peer_to(r, d, nr), c), device_id_type=MESH,
        )

    def forward(block, factor):
        right = (high[...], low[...])
        one = dot3(split(fock[0, at(block), :]), right)
        two = dot3(split(fock[1, at(block), :]), right)
        real = one[:, :m] - two[:, m:]
        imag = one[:, m:] + two[:, :m]
        piece = nc * r + block
        weight = jnp.where(lax.div(piece, nr) == c, 1.0, 0.0).astype(jnp.float32)
        own = base[at(lax.rem(piece, nr)), :] * weight
        return own[:, :m] - factor * imag, own[:, m:] + factor * real

    def forward_reduce(factor, load, send, recv, ssem, rsem):
        def product(e, target):
            if load:
                fock_load(e).wait()
            real, imag = forward(block_to(e), factor)
            target[e, :, :m] = real
            target[e, :, m:] = imag

        def partial_copy(e):
            return col_copy(e, near(e), send.at[e], recv, ssem, rsem)

        def sum_copy():
            return col_copy(half - 1, across, recv.at[half - 1], send, ssem, rsem)

        def step(e):
            product(e, send)
            partial_copy(e).start()

        def take(e, total):
            partial_copy(e).wait_recv()
            recv[total] += recv[e]

        each(half - 1, step)
        product(half - 1, recv)
        each(half - 1, lambda d: step(half + d))
        product(nc - 1, recv)
        each(half - 1, lambda d: take(d, half - 1))
        sum_copy().start()
        each(half - 1, lambda d: take(half + d, nc - 1))
        sum_copy().wait_recv()
        recv[nc - 1] += send[half - 1]

        def drain():
            each(half - 1, lambda d: partial_copy(d).wait_send())
            each(half - 1, lambda d: partial_copy(half + d).wait_send())
            sum_copy().wait_send()

        return drain

    drain1 = forward_reduce(time_step, True, send1, recv1, s1, r1)

    gather1[nc - 1] = recv1[nc - 1]
    def across_copy():
        return col_copy(half - 1, across, gather1.at[nc - 1], gather1, s2, r2)

    def near_copy(d):
        return col_copy(half + d, near(d), gather1.at[nc - 1], gather1, s2, r2)

    def forward_copy(d):
        return col_copy(d, near(d), gather1.at[half - 1], gather1, s2, r2)

    across_copy().start()
    each(half - 1, lambda d: near_copy(d).start())

    def backward(e):
        density_load(e).wait()
        block = block_from(e)
        left = split(gather1[e].T)
        one = dot3(left, split(density[0, at(block), :]))
        two = dot3(left, split(density[1, at(block), :]))
        return one[:m] + two[m:], one[m:] - two[:m]

    real, imag = backward(nc - 1)
    turned[:m] = real
    turned[m:] = imag

    across_copy().wait_recv()
    each(half - 1, lambda d: forward_copy(d).start())

    def add_backward(e):
        real, imag = backward(e)
        turned[:m] += real
        turned[m:] += imag

    def gathered_near(d):
        near_copy(d).wait_recv()
        add_backward(half + d)

    def gathered_far(d):
        forward_copy(d).wait_recv()
        add_backward(d)

    add_backward(half - 1)
    each(half - 1, gathered_near)
    each(half - 1, gathered_far)
    flat[...] = turned[...].T

    each(nr - 1, lambda d: row_copy(d, flat.at[at(peer_to(r, d, nr)), :], recv2, s3, r3).start())
    recv2[nr - 1] = flat[at(r), :]

    def take_row(d):
        row_copy(d, flat.at[at(peer_to(r, d, nr)), :], recv2, s3, r3).wait_recv()
        recv2[nr - 1] += recv2[d]

    each(nr - 1, take_row)

    gather2[nr - 1] = recv2[nr - 1]
    each(nr - 1, lambda d: row_copy(d, gather2.at[nr - 1], gather2, s4, r4).start())

    def place(slot):
        value = gather2[slot]
        where = at(peer_from(r, slot, nr))
        top, rest = split(value)
        base[where, :] = value
        high[where, :] = top
        low[where, :] = rest

    place(nr - 1)

    def take_vector(d):
        row_copy(d, gather2.at[nr - 1], gather2, s4, r4).wait_recv()
        place(d)

    each(nr - 1, take_vector)

    drain3 = forward_reduce(-time_step, False, send3, recv3, s5, r5)

    moved[...] = recv3[nc - 1]

    def move():
        return pltpu.make_async_remote_copy(
            src_ref=moved, dst_ref=gather4.at[nr - 1], send_sem=s6.at[0], recv_sem=r6.at[0],
            device_id=goal, device_id_type=MESH,
        )

    def stay():
        return pltpu.make_async_copy(moved, gather4.at[nr - 1], own_sem.at[0])

    @pl.when(stays)
    def _():
        stay().start()
        stay().wait()

    @pl.when(jnp.logical_not(stays))
    def _():
        move().start()
        move().wait()

    each(nr - 1, lambda d: row_copy(d, gather4.at[nr - 1], gather4, s7, r7).start())

    def emit(slot):
        where = at(peer_from(r, slot, nr))
        out_ref[0, where, :] = gather4[slot, :, :m]
        out_ref[1, where, :] = gather4[slot, :, m:]

    emit(nr - 1)

    def take_out(d):
        row_copy(d, gather4.at[nr - 1], gather4, s7, r7).wait_recv()
        emit(d)

    each(nr - 1, take_out)

    drain1()
    drain3()
    across_copy().wait_send()
    each(half - 1, lambda d: near_copy(d).wait_send())
    each(half - 1, lambda d: forward_copy(d).wait_send())

    def drain_row(d):
        row_copy(d, flat.at[at(peer_to(r, d, nr)), :], recv2, s3, r3).wait_send()
        row_copy(d, gather2.at[nr - 1], gather2, s4, r4).wait_send()
        row_copy(d, gather4.at[nr - 1], gather4, s7, r7).wait_send()

    each(nr - 1, drain_row)


def solution(mesh):
    nr = mesh.shape["row"]
    nc = mesh.shape["col"]

    def shards(fock, density, probe):
        _, rows, cols = fock.shape
        m = probe.shape[2]
        s = rows // nc
        f32 = jnp.float32
        vmem = pltpu.VMEM
        sem = pltpu.SemaphoreType.DMA
        many, few = (nc, s, 2 * m), (nr, s, 2 * m)
        return pl.pallas_call(
            functools.partial(kernel, nr, nc),
            out_shape=jax.ShapeDtypeStruct(probe.shape, f32),
            in_specs=[
                pl.BlockSpec(memory_space=pl.ANY),
                pl.BlockSpec(memory_space=pl.ANY),
                pl.BlockSpec(memory_space=pltpu.VMEM),
            ],
            out_specs=pl.BlockSpec(memory_space=pltpu.VMEM),
            scratch_shapes=[
                vmem(fock.shape, f32),
                vmem(density.shape, f32),
                vmem((cols, 2 * m), jnp.bfloat16),
                vmem((cols, 2 * m), jnp.bfloat16),
                vmem((cols, 2 * m), f32),
                vmem(many, f32),
                vmem(many, f32),
                vmem(many, f32),
                vmem((2 * m, cols), f32),
                vmem((cols, 2 * m), f32),
                vmem(few, f32),
                vmem(few, f32),
                vmem(many, f32),
                vmem(many, f32),
                vmem((s, 2 * m), f32),
                vmem(few, f32),
                sem((nc,)),
                sem((nc,)),
                sem((1,)),
                *[sem((nc,))] * 14,
            ],
            compiler_params=pltpu.CompilerParams(
                collective_id=0, has_side_effects=True, vmem_limit_bytes=62 * 1024 * 1024
            ),
            name="propagate",
        )(fock, density, probe)

    return jax.shard_map(
        shards,
        mesh=mesh,
        in_specs=(P(None, "row", "col"), P(None, "row", "col"), P(None, "col", None)),
        out_specs=P(None, "col", None),
        check_vma=False,
    )
```
